512 devices in a mesh: layer: 2 (over y_lo), feat: 64 (over y_hi, z, core), width: 4 (over x).
Axes of the slice: x: 4, y: 4 (y_hi: 2, y_lo: 2; y = y_hi * 2 + y_lo), z: 16, core: 2. Of those that a mesh axis runs over, the one named last changes fastest.
Arguments:
- inputs: float32 [2, 1024, 2048], P('layer', None, 'width'), may hold values from -6 to 6
- targets: float32 [2, 1024, 2048], P(None, ('layer', 'feat'), 'width'), may hold values from -6 to 6
- w_enc: float32 [2, 2048, 16384], P('layer', 'width', 'feat'), may hold values from -0.125 to 0.125
- b_enc: float32 [2, 16384], P('layer', 'feat'), may hold values from -3 to 3
- thresholds: float32 [2, 16384], P('layer', 'feat'), may hold values from 0.2 to 1
- w_dec: float32 [2, 2, 16384, 2048], P('layer', None, 'feat', 'width'), may hold values from -0.046875 to 0.046875
- b_dec: float32 [2, 2048], P(None, 'width'), may hold values from -3 to 3
Outputs:
- dec_grad: float32 [2, 2, 16384, 2048], P('layer', None, 'feat', 'width')
- pre_grad: float32 [2, 1024, 16384], P('layer', 'width', 'feat')
The draws below stay inside these ranges and needn't reach their ends.
All inputs are finite; a program needn't handle non-finite values.
Results may differ from the reference program's by a relative error of at most 0.0001.
Values sent between devices are 32-bit elements; how exact they have to be, the bound alone decides.
A program may use at most 64 MiB of HBM per device.

```python
import jax
import jax.numpy as jnp
from jax import lax

D = 2048
F = 16384
TOK = 1024
LAYERS = 2


def level_of(stream_key, shape, shards, smallest, largest):
    gain = 1.0
    for dim, blocks in shards:
        draws = jax.random.uniform(jax.random.fold_in(jax.random.fold_in(stream_key, 6), dim), (blocks,), jnp.float32, smallest / len(shards), largest / len(shards))
        gain = gain * jnp.repeat(jnp.exp(draws), shape[dim] // blocks).reshape((-1,) + (1,) * (len(shape) - 1 - dim))
    return gain


def noise(own_key, extent, width, limit, cuts=(), kind=jnp.bfloat16):
    level = level_of(own_key, extent, cuts, -0.22, 0.18) if cuts else 1.0
    array = jax.random.normal(own_key, extent, jnp.float32) * width * level
    return jnp.minimum(jnp.maximum(array, -limit), limit).astype(kind)


def setup_inputs(seed: int = 0) -> dict:
    streams_of = jax.random.split(jax.random.key(seed), 8)
    return {
        "inputs": noise(streams_of[0], (LAYERS, TOK, D), 1.0, 6.0, ((0, 2), (2, 4)), jnp.float32),
        "targets": noise(streams_of[1], (LAYERS, TOK, D), 1.0, 6.0, ((1, 128), (2, 4)), jnp.float32),
        "w_enc": noise(streams_of[2], (LAYERS, D, F), D ** -0.5, 0.125, ((0, 2), (1, 4), (2, 64)), jnp.float32),
        "b_enc": noise(streams_of[3], (LAYERS, F), 0.5, 3.0, ((0, 2), (1, 64)), jnp.float32),
        "thresholds": jnp.clip(0.2 + 0.8 * jax.random.uniform(streams_of[4], (LAYERS, F), jnp.float32) ** level_of(streams_of[4], (LAYERS, F), ((0, 2), (1, 64)), -0.2, 0.2), 0.2, 1.0),
        "w_dec": noise(streams_of[5], (LAYERS, LAYERS, F, D), F ** -0.5, 0.046875, ((0, 2), (2, 64), (3, 4)), jnp.float32),
        "b_dec": noise(streams_of[6], (LAYERS, D), 0.5, 3.0, ((1, 4),), jnp.float32),
    }


softness = 0.5


def reference(inputs, targets, w_enc, b_enc, thresholds, w_dec, b_dec):
    highest = lax.Precision.HIGHEST
    pre_act = jnp.einsum('lnd,ldf->lnf', inputs, w_enc, precision=highest) + b_enc[:, None, :]
    gate_open = jax.nn.sigmoid((pre_act - thresholds[:, None, :]) / softness)
    activations = pre_act * gate_open
    slope_val = gate_open + pre_act * gate_open * (1.0 - gate_open) / softness
    errors = []
    for target_pos in range(LAYERS):
        recon = b_dec[target_pos][None, :] - targets[target_pos]
        for source_pos in range(target_pos + 1):
            recon = recon + jnp.dot(activations[source_pos], w_dec[source_pos, target_pos], precision=highest, preferred_element_type=jnp.float32)
        errors.append(recon)
    grad_rows = []
    back_rows = []
    for source_pos in range(LAYERS):
        per_target = []
        back_sum = jnp.zeros(activations.shape[1:], activations.dtype)
        for target_pos in range(LAYERS):
            if target_pos >= source_pos:
                per_target.append(lax.dot_general(activations[source_pos], errors[target_pos], (((0,), (0,)), ((), ())), precision=highest, preferred_element_type=jnp.float32))
                back_sum = back_sum + lax.dot_general(errors[target_pos], w_dec[source_pos, target_pos], (((1,), (1,)), ((), ())), precision=highest, preferred_element_type=jnp.float32)
            else:
                per_target.append(jnp.zeros(w_dec.shape[2:], w_dec.dtype))
        grad_rows.append(jnp.stack(per_target))
        back_rows.append(back_sum * slope_val[source_pos])
    return jnp.stack(grad_rows), jnp.stack(back_rows)
```

```python
import functools

import jax
import jax.numpy as jnp
from jax import lax
from jax.experimental import pallas as pl
from jax.experimental.pallas import tpu as pltpu
from jax.sharding import PartitionSpec as P

softness = 0.5
MESH = pl.DeviceIdType.MESH
CHUNKS = 4
NX = 4
NY = 4
NZ = 16
F32 = jnp.float32
BF16 = jnp.bfloat16

STAGES = (
    ("pre", 1.5),
    ("gate", 5.5),
    ("recon", 5.5),
    ("core_sum", 2.5),
    ("y_sum", 7.5),
    ("zlo_sum", 6.0),
    ("zhi_sum", 8.0),
    ("zhi_all", 8.0),
    ("zlo_all", 6.0),
    ("y_all", 7.5),
    ("back", 2.5),
    ("grad", 0.3),
    ("finish", 5.5),
)


def stage_order(chunks):
    ready = []
    for chunk in range(chunks):
        when = chunk * 4.0
        for place, (name, wait) in enumerate(STAGES):
            when += wait
            ready.append((when, place, chunk, name))
    return [(name, chunk) for _, _, chunk, name in sorted(ready)]


def split(value):
    high = value.astype(BF16)
    low = (value - high.astype(F32)).astype(BF16)
    return high, low


def product(a, b, dims):
    dot = functools.partial(
        lax.dot_general, dimension_numbers=(dims, ((), ())), preferred_element_type=F32
    )
    return dot(a[0], b[0]) + (dot(a[0], b[1]) + dot(a[1], b[0]))


NN = ((1,), (0,))
NT = ((1,), (1,))


def kernel(
    x_hbm,
    targets_ref,
    enc_hbm,
    b_enc_ref,
    thr_ref,
    dec_hbm,
    b_dec_ref,
    dec_grad_ref,
    pre_grad_ref,
    x_ref,
    enc_f32,
    dec_f32,
    enc,
    dec,
    pre_part,
    pre_recv,
    acts,
    slope,
    q_send,
    q_own,
    q_recv,
    y_recv,
    zlo_part,
    zlo_recv,
    zhi_part,
    zhi_recv,
    errs,
    back_part,
    back_recv,
    load_sem,
    x_ss,
    x_rs,
    y_ss,
    y_rs,
    zlo_ss,
    zlo_rs,
    zhi_ss,
    zhi_rs,
    c_ss,
    c_rs,
):
    layer = lax.axis_index("layer")
    feat = lax.axis_index("feat")
    width = lax.axis_index("width")
    core = lax.rem(feat, 2)
    z = lax.rem(feat // 2, NZ)
    zlo = lax.rem(z, 4)
    zhi = z // 4
    y = (feat // (2 * NZ)) * 2 + layer
    chunks, _, rows, _ = acts.shape
    block = 2 * rows // NZ

    def turn(place, step):
        return lax.rem(place + step, 4)

    def device(y_at, z_at, core_at, x_at):
        return (lax.rem(y_at, 2), (y_at // 2) * (2 * NZ) + z_at * 2 + core_at, x_at)

    def x_peer(step):
        return device(y, z, core, turn(width, step))

    def y_peer(step):
        return device(turn(y, step), z, core, width)

    def zlo_peer(step):
        return device(y, zhi * 4 + turn(zlo, step), core, width)

    def zhi_peer(step):
        return device(y, turn(zhi, step) * 4 + zlo, core, width)

    partner = device(y, z, 1 - core, width)
    peers = [partner] + [peer(step) for peer in (x_peer, y_peer, zlo_peer, zhi_peer) for step in (1, 2, 3)]

    loads = [
        pltpu.make_async_copy(enc_hbm, enc_f32, load_sem.at[0]),
        pltpu.make_async_copy(x_hbm, x_ref, load_sem.at[1]),
        pltpu.make_async_copy(dec_hbm, dec_f32, load_sem.at[2]),
    ]
    for load in loads:
        load.start()
    barrier = pltpu.get_barrier_semaphore()
    for peer in peers:
        pl.semaphore_signal(barrier, inc=1, device_id=peer, device_id_type=MESH)

    sent = []

    def send(src, dst, send_sem, recv_sem, peer):
        copy = pltpu.make_async_remote_copy(
            src_ref=src,
            dst_ref=dst,
            send_sem=send_sem,
            recv_sem=recv_sem,
            device_id=peer,
            device_id_type=MESH,
        )
        copy.start()
        sent.append(copy)
        return copy

    pending = {}

    def arrive(key):
        for copy in pending.pop(key):
            copy.wait_recv()

    loads[0].wait()
    high, low = split(enc_f32[...])
    enc[0] = high
    enc[1] = low
    loads[1].wait()
    pl.semaphore_wait(barrier, len(peers))

    def load_dec():
        loads[2].wait()
        for target in range(2):
            for half in range(2):
                value = dec_f32[target, :, half * 256 : (half + 1) * 256]
                if target == 0:
                    value = jnp.where(layer == 0, value, 0.0)
                high, low = split(value)
                dec[half, target, 0] = high
                dec[half, target, 1] = low

    def pre(c):
        value = x_ref[:, c].reshape(4 * rows, x_ref.shape[3])
        part = product(split(value), (enc[0], enc[1]), NN)
        pre_part[c] = part.reshape(4, rows, 256)
        pending["pre", c] = [
            send(
                pre_part.at[c, turn(width, step)],
                pre_recv.at[c, step - 1],
                x_ss.at[0, c, step - 1],
                x_rs.at[0, c, step - 1],
                x_peer(step),
            )
            for step in (1, 3, 2)
        ]
        if c == 0:
            load_dec()

    def gate(c):
        arrive(("pre", c))
        total = pre_part[c, width] + pre_recv[c, 0] + pre_recv[c, 1] + pre_recv[c, 2]
        total = total + b_enc_ref[...]
        opened = jax.nn.sigmoid((total - thr_ref[...]) / softness)
        acts[c, width] = total * opened
        slope[c] = opened + total * opened * (1.0 - opened) / softness
        pending["acts", c] = [
            send(
                acts.at[c, width],
                acts.at[c, width],
                x_ss.at[1, c, step - 1],
                x_rs.at[1, c, step - 1],
                x_peer(step),
            )
            for step in (1, 3, 2)
        ]

    first = (layer * 64 + feat) * targets_ref.shape[1]
    own_x = first // (rows * chunks)
    own_chunk = lax.rem(first, rows * chunks) // rows
    own_row = pl.multiple_of(lax.rem(first, rows), 8)

    def recon(c):
        arrive(("acts", c))
        value = split(acts[c].reshape(4 * rows, 256))
        for dst, half in ((q_send, 1 - core), (q_own, core)):
            for target in range(2):
                part = product(value, (dec[half, target, 0], dec[half, target, 1]), NN)
                dst[c, :, target * rows : (target + 1) * rows, :] = part.reshape(4, rows, 256)

            @pl.when(own_chunk == c)
            def _():
                for target in range(2):
                    at = pl.multiple_of(target * rows + own_row, 8)
                    spot = (c, own_x, pl.ds(at, 8), slice(None))
                    columns = pl.ds(pl.multiple_of(half * 256, 256), 256)
                    dst[spot] = dst[spot] - targets_ref[target, :, columns]

            if dst is q_send:
                pending["q", c] = [
                    send(q_send.at[c], q_recv.at[c], c_ss.at[0, c], c_rs.at[0, c], partner)
                ]

    def core_sum(c):
        arrive(("q", c))
        copies = []
        for step in (1, 3, 2):
            at = turn(y, step)
            q_own[c, at] = q_own[c, at] + q_recv[c, at]
            copies.append(
                send(
                    q_own.at[c, at],
                    y_recv.at[c, step - 1],
                    y_ss.at[0, c, step - 1],
                    y_rs.at[0, c, step - 1],
                    y_peer(step),
                )
            )
        pending["y", c] = copies

    def y_sum(c):
        arrive(("y", c))
        total = (q_own[c, y] + q_recv[c, y]) + (y_recv[c, 0] + y_recv[c, 1] + y_recv[c, 2])
        zlo_part[c] = total.reshape(4, 4 * block, 256)
        pending["zlo", c] = [
            send(
                zlo_part.at[c, turn(zlo, step)],
                zlo_recv.at[c, step - 1],
                zlo_ss.at[0, c, step - 1],
                zlo_rs.at[0, c, step - 1],
                zlo_peer(step),
            )
            for step in (1, 3, 2)
        ]

    def zlo_sum(c):
        arrive(("zlo", c))
        total = zlo_part[c, zlo] + (zlo_recv[c, 0] + zlo_recv[c, 1] + zlo_recv[c, 2])
        zhi_part[c] = total.reshape(4, block, 256)
        pending["zhi", c] = [
            send(
                zhi_part.at[c, turn(zhi, step)],
                zhi_recv.at[c, step - 1],
                zhi_ss.at[0, c, step - 1],
                zhi_rs.at[0, c, step - 1],
                zhi_peer(step),
            )
            for step in (2, 1, 3)
        ]

    def zhi_sum(c):
        arrive(("zhi", c))
        total = zhi_part[c, zhi] + (zhi_recv[c, 0] + zhi_recv[c, 1] + zhi_recv[c, 2])
        columns = pl.ds(pl.multiple_of(core * 256, 256), 256)
        bias = b_dec_ref[:, columns]
        total = total + jnp.where(zlo >= 2, bias[1:2], bias[0:1])
        errs[c, core, y, zlo, zhi] = total
        own = errs.at[c, core, y, zlo, zhi]
        pending["zhi_all", c] = [
            send(own, own, zhi_ss.at[1, c, step - 1], zhi_rs.at[1, c, step - 1], zhi_peer(step))
            for step in (2, 1, 3)
        ]

    def zhi_all(c):
        arrive(("zhi_all", c))
        own = errs.at[c, core, y, zlo]
        pending["zlo_all", c] = [
            send(own, own, zlo_ss.at[1, c, step - 1], zlo_rs.at[1, c, step - 1], zlo_peer(step))
            for step in (1, 3, 2)
        ]

    def zlo_all(c):
        arrive(("zlo_all", c))
        own = errs.at[c, core, y]
        pending["y_all", c] = [
            send(own, own, y_ss.at[1, c, step - 1], y_rs.at[1, c, step - 1], y_peer(step))
            for step in (1, 3, 2)
        ]

    def y_all(c):
        arrive(("y_all", c))
        own = errs.at[c, core]
        pending["e", c] = [send(own, own, c_ss.at[1, c], c_rs.at[1, c], partner)]

    def error_of(c, half, target):
        value = errs[c, half].reshape(4, 2 * rows, 256)
        return value[:, target * rows : (target + 1) * rows].reshape(4 * rows, 256)

    def back(c):
        arrive(("e", c))
        total = None
        for half in range(2):
            for target in range(2):
                value = split(error_of(c, half, target))
                part = product(value, (dec[half, target, 0], dec[half, target, 1]), NT)
                total = part if total is None else total + part
        back_part[c] = total.reshape(4, rows, 256)
        pending["back", c] = [
            send(
                back_part.at[c, turn(width, step)],
                back_recv.at[c, step - 1],
                x_ss.at[2, c, step - 1],
                x_rs.at[2, c, step - 1],
                x_peer(step),
            )
            for step in (1, 3, 2)
        ]

    def grad(c):
        turned = split(acts[c].reshape(4 * rows, 256).T)
        for target in range(2):
            for half in range(2):
                part = product(turned, split(error_of(c, half, target)), NN)
                if target == 0:
                    part = jnp.where(layer == 0, part, 0.0)
                columns = slice(half * 256, (half + 1) * 256)
                if c == 0:
                    dec_grad_ref[target, :, columns] = part
                else:
                    dec_grad_ref[target, :, columns] += part

    def finish(c):
        arrive(("back", c))
        total = back_part[c, width] + (back_recv[c, 0] + back_recv[c, 1] + back_recv[c, 2])
        pre_grad_ref[c * rows : (c + 1) * rows, :] = total * slope[c]

    run = locals()
    stages = {name: run[name] for name, _ in STAGES}
    for name, c in stage_order(chunks):
        stages[name](c)
    for copy in sent:
        copy.wait_send()


def local(inputs, targets, w_enc, b_enc, thresholds, w_dec, b_dec):
    tokens, width = inputs.shape[1:]
    feats = w_enc.shape[2]
    c = CHUNKS
    rows = tokens // (NX * c)
    block = 2 * rows // NZ
    half = width // 2
    vmem = pl.BlockSpec(memory_space=pltpu.VMEM)
    anywhere = pl.BlockSpec(memory_space=pl.ANY)
    dma = pltpu.SemaphoreType.DMA
    dec_grad, pre_grad = pl.pallas_call(
        kernel,
        out_shape=(
            jax.ShapeDtypeStruct(w_dec.shape[1:], F32),
            jax.ShapeDtypeStruct((tokens // NX, feats), F32),
        ),
        in_specs=[anywhere, vmem, anywhere, vmem, vmem, anywhere, vmem],
        out_specs=(vmem, vmem),
        scratch_shapes=[
            pltpu.VMEM((NX, c, rows, width), F32),
            pltpu.VMEM((width, feats), F32),
            pltpu.VMEM((2, feats, width), F32),
            pltpu.VMEM((2, width, feats), BF16),
            pltpu.VMEM((2, 2, 2, feats, half), BF16),
            pltpu.VMEM((c, NX, rows, feats), F32),
            pltpu.VMEM((c, 3, rows, feats), F32),
            pltpu.VMEM((c, NX, rows, feats), F32),
            pltpu.VMEM((c, rows, feats), F32),
            pltpu.VMEM((c, NY, 2 * rows, half), F32),
            pltpu.VMEM((c, NY, 2 * rows, half), F32),
            pltpu.VMEM((c, NY, 2 * rows, half), F32),
            pltpu.VMEM((c, 3, 2 * rows, half), F32),
            pltpu.VMEM((c, 4, 4 * block, half), F32),
            pltpu.VMEM((c, 3, 4 * block, half), F32),
            pltpu.VMEM((c, 4, block, half), F32),
            pltpu.VMEM((c, 3, block, half), F32),
            pltpu.VMEM((c, 2, NY, 4, 4, block, half), F32),
            pltpu.VMEM((c, NX, rows, feats), F32),
            pltpu.VMEM((c, 3, rows, feats), F32),
            dma((3,)),
            dma((3, c, 3)),
            dma((3, c, 3)),
            dma((2, c, 3)),
            dma((2, c, 3)),
            dma((2, c, 3)),
            dma((2, c, 3)),
            dma((2, c, 3)),
            dma((2, c, 3)),
            dma((2, c)),
            dma((2, c)),
        ],
        compiler_params=pltpu.CompilerParams(
            collective_id=0, has_side_effects=True, vmem_limit_bytes=60 * 1024 * 1024
        ),
    )(
        inputs.reshape(NX, c, rows, width),
        targets,
        w_enc[0],
        b_enc,
        thresholds,
        w_dec[0],
        b_dec,
    )
    return dec_grad[None], pre_grad[None]


def solution(mesh):
    in_specs = (
        P("layer", None, "width"),
        P(None, ("layer", "feat"), "width"),
        P("layer", "width", "feat"),
        P("layer", "feat"),
        P("layer", "feat"),
        P("layer", None, "feat", "width"),
        P(None, "width"),
    )
    out_specs = (P("layer", None, "feat", "width"), P("layer", "width", "feat"))
    return jax.shard_map(local, mesh=mesh, in_specs=in_specs, out_specs=out_specs, check_vma=False)
```

```python
import functools

import jax
import jax.numpy as jnp
from jax import lax
from jax.experimental import pallas as pl
from jax.experimental.pallas import tpu as pltpu
from jax.sharding import PartitionSpec as P

softness = 0.5
MESH = pl.DeviceIdType.MESH
CHUNKS = 8
SPACING = 3.5
NX = 4
NY = 4
NZ = 16
F32 = jnp.float32
BF16 = jnp.bfloat16

STAGES = (
    ("pre", 1.5),
    ("gate", 4.5),
    ("recon", 4.5),
    ("core_sum", 1.8),
    ("y_sum", 5.3),
    ("zlo_sum", 5.1),
    ("zhi_sum", 7.5),
    ("zhi_all", 7.5),
    ("zlo_all", 5.1),
    ("y_all", 5.3),
    ("back", 1.8),
    ("grad", 0.3),
    ("finish", 4.5),
)


def stage_order(chunks):
    ready = []
    for chunk in range(chunks):
        when = chunk * SPACING
        for place, (name, wait) in enumerate(STAGES):
            when += wait
            ready.append((when, place, chunk, name))
    return [(name, chunk) for _, _, chunk, name in sorted(ready)]


def split(value):
    high = value.astype(BF16)
    low = (value - high.astype(F32)).astype(BF16)
    return high, low


def product(a, b, dims):
    dot = functools.partial(
        lax.dot_general, dimension_numbers=(dims, ((), ())), preferred_element_type=F32
    )
    return dot(a[0], b[0]) + (dot(a[0], b[1]) + dot(a[1], b[0]))


NN = ((1,), (0,))
NT = ((1,), (1,))


def kernel(
    x_hbm,
    targets_hbm,
    enc_hbm,
    b_enc_hbm,
    thr_hbm,
    dec_hbm,
    b_dec_hbm,
    dec_grad_ref,
    pre_grad_ref,
    targets_ref,
    b_enc_ref,
    thr_ref,
    b_dec_ref,
    x_ref,
    enc_f32,
    dec_f32,
    enc,
    dec,
    pre_part,
    pre_recv,
    acts,
    slope,
    q_send,
    q_own,
    q_recv,
    y_recv,
    zlo_part,
    zlo_recv,
    zhi_part,
    zhi_recv,
    errs,
    back_part,
    back_recv,
    load_sem,
    x_ss,
    x_rs,
    y_ss,
    y_rs,
    zlo_ss,
    zlo_rs,
    zhi_ss,
    zhi_rs,
    c_ss,
    c_rs,
):
    layer = lax.axis_index("layer")
    feat = lax.axis_index("feat")
    width = lax.axis_index("width")
    core = lax.rem(feat, 2)
    z = lax.rem(feat // 2, NZ)
    zlo = lax.rem(z, 4)
    zhi = z // 4
    y = (feat // (2 * NZ)) * 2 + layer
    chunks, _, rows, _ = acts.shape

    def turn(place, step):
        return lax.rem(place + step, 4)

    def device(y_at, z_at, core_at, x_at):
        return (lax.rem(y_at, 2), (y_at // 2) * (2 * NZ) + z_at * 2 + core_at, x_at)

    def x_peer(step):
        return device(y, z, core, turn(width, step))

    def y_peer(step):
        return device(turn(y, step), z, core, width)

    def zlo_peer(step):
        return device(y, zhi * 4 + turn(zlo, step), core, width)

    def zhi_peer(step):
        return device(y, turn(zhi, step) * 4 + zlo, core, width)

    partner = device(y, z, 1 - core, width)
    peers = [partner] + [peer(step) for peer in (x_peer, y_peer, zlo_peer, zhi_peer) for step in (1, 2, 3)]

    loads = [
        pltpu.make_async_copy(enc_hbm, enc_f32, load_sem.at[0]),
        pltpu.make_async_copy(dec_hbm, dec_f32, load_sem.at[1]),
    ]
    x_loads = [
        pltpu.make_async_copy(x_hbm.at[:, c], x_ref.at[:, c], load_sem.at[2 + c]) for c in range(chunks)
    ]
    small = ((b_enc_hbm, b_enc_ref), (thr_hbm, thr_ref), (targets_hbm, targets_ref), (b_dec_hbm, b_dec_ref))
    small_loads = [
        pltpu.make_async_copy(src, dst, load_sem.at[2 + chunks + place]) for place, (src, dst) in enumerate(small)
    ]
    for load in [loads[0], x_loads[0], *small_loads, loads[1], *x_loads[1:]]:
        load.start()
    barrier = pltpu.get_barrier_semaphore()
    for peer in peers:
        pl.semaphore_signal(barrier, inc=1, device_id=peer, device_id_type=MESH)

    sent = []

    def send(src, dst, send_sem, recv_sem, peer):
        copy = pltpu.make_async_remote_copy(
            src_ref=src,
            dst_ref=dst,
            send_sem=send_sem,
            recv_sem=recv_sem,
            device_id=peer,
            device_id_type=MESH,
        )
        copy.start()
        sent.append(copy)
        return copy

    pending = {}

    def arrive(key):
        for copy in pending.pop(key):
            copy.wait_recv()

    loads[0].wait()
    high, low = split(enc_f32[...])
    enc[0] = high
    enc[1] = low

    def load_dec():
        for target in range(2):
            for half in range(2):
                value = dec_f32[target, :, half * 256 : (half + 1) * 256]
                if target == 0:
                    value = jnp.where(layer == 0, value, 0.0)
                high, low = split(value)
                dec[half, target, 0] = high
                dec[half, target, 1] = low

    def pre(c):
        x_loads[c].wait()
        value = x_ref[:, c].reshape(4 * rows, x_ref.shape[3])
        part = product(split(value), (enc[0], enc[1]), NN)
        pre_part[c] = part.reshape(4, rows, 256)
        if c == 0:
            pl.semaphore_wait(barrier, len(peers))
        pending["pre", c] = [
            send(
                pre_part.at[c, turn(width, step)],
                pre_recv.at[c, step - 1],
                x_ss.at[0, c, step - 1],
                x_rs.at[0, c, step - 1],
                x_peer(step),
            )
            for step in (1, 3, 2)
        ]
        if c == 0:
            loads[1].wait()
            for load in small_loads:
                load.wait()
            load_dec()

    def gate(c):
        arrive(("pre", c))
        total = pre_part[c, width] + pre_recv[c, 0] + pre_recv[c, 1] + pre_recv[c, 2]
        total = total + b_enc_ref[...]
        opened = jax.nn.sigmoid((total - thr_ref[...]) / softness)
        acts[c, width] = total * opened
        slope[c] = opened + total * opened * (1.0 - opened) / softness
        pending["acts", c] = [
            send(
                acts.at[c, width],
                acts.at[c, width],
                x_ss.at[1, c, step - 1],
                x_rs.at[1, c, step - 1],
                x_peer(step),
            )
            for step in (1, 3, 2)
        ]

    first = (layer * 64 + feat) * targets_ref.shape[1]
    own_x = first // (rows * chunks)
    own_chunk = lax.rem(first, rows * chunks) // rows
    own_row = pl.multiple_of(lax.rem(first, rows), 8)

    def recon(c):
        arrive(("acts", c))
        value = split(acts[c].reshape(4 * rows, 256))
        for dst, half in ((q_send, 1 - core), (q_own, core)):
            for target in range(2):
                part = product(value, (dec[half, target, 0], dec[half, target, 1]), NN)
                dst[c, :, target * rows : (target + 1) * rows, :] = part.reshape(4, rows, 256)

            @pl.when(own_chunk == c)
            def _():
                for target in range(2):
                    at = pl.multiple_of(target * rows + own_row, 8)
                    spot = (c, own_x, pl.ds(at, 8), slice(None))
                    columns = pl.ds(pl.multiple_of(half * 256, 256), 256)
                    dst[spot] = dst[spot] - targets_ref[target, :, columns]

            if dst is q_send:
                pending["q", c] = [
                    send(q_send.at[c], q_recv.at[c], c_ss.at[0, c, 0], c_rs.at[0, c, 0], partner)
                ]

    def core_sum(c):
        arrive(("q", c))
        copies = []
        for step in (1, 3, 2):
            at = turn(y, step)
            q_own[c, at] = q_own[c, at] + q_recv[c, at]
            copies.append(
                send(
                    q_own.at[c, at],
                    y_recv.at[c, step - 1],
                    y_ss.at[0, c, step - 1],
                    y_rs.at[0, c, step - 1],
                    y_peer(step),
                )
            )
        pending["y", c] = copies

    def y_sum(c):
        arrive(("y", c))
        total = (q_own[c, y] + q_recv[c, y]) + (y_recv[c, 0] + y_recv[c, 1] + y_recv[c, 2])
        zlo_part[c] = total.reshape(4, 2 * rows // 4, 256)
        pending["zlo", c] = [
            send(
                zlo_part.at[c, turn(zlo, step)],
                zlo_recv.at[c, step - 1],
                zlo_ss.at[0, c, step - 1],
                zlo_rs.at[0, c, step - 1],
                zlo_peer(step),
            )
            for step in (1, 3, 2)
        ]

    def zlo_sum(c):
        arrive(("zlo", c))
        total = zlo_part[c, zlo] + (zlo_recv[c, 0] + zlo_recv[c, 1] + zlo_recv[c, 2])
        for part in range(4):
            down, across = (part // 2) * 8, (part % 2) * 128
            zhi_part[c, part] = total[down : down + 8, across : across + 128]
        pending["zhi", c] = [
            send(
                zhi_part.at[c, turn(zhi, step)],
                zhi_recv.at[c, step - 1],
                zhi_ss.at[0, c, step - 1],
                zhi_rs.at[0, c, step - 1],
                zhi_peer(step),
            )
            for step in (2, 1, 3)
        ]

    def zhi_sum(c):
        arrive(("zhi", c))
        total = zhi_part[c, zhi] + (zhi_recv[c, 0] + zhi_recv[c, 1] + zhi_recv[c, 2])
        columns = pl.ds(pl.multiple_of(core * 256 + lax.rem(zhi, 2) * 128, 128), 128)
        bias = b_dec_ref[:, columns]
        total = total + jnp.where(zlo >= 2, bias[1:2], bias[0:1])
        errs[c, core, y, zlo, zhi] = total
        own = errs.at[c, core, y, zlo, zhi]
        pending["zhi_all", c] = [
            send(own, own, zhi_ss.at[1, c, step - 1], zhi_rs.at[1, c, step - 1], zhi_peer(step))
            for step in (2, 1, 3)
        ]

    def zhi_all(c):
        arrive(("zhi_all", c))
        own = errs.at[c, core, y, zlo]
        pending["zlo_all", c] = [
            send(own, own, zlo_ss.at[1, c, step - 1], zlo_rs.at[1, c, step - 1], zlo_peer(step))
            for step in (1, 3, 2)
        ]

    def pass_on(c, at):
        own = errs.at[c, core, at]
        return send(own, own, c_ss.at[1, c, at], c_rs.at[1, c, at], partner)

    def zlo_all(c):
        arrive(("zlo_all", c))
        own = errs.at[c, core, y]
        pending["y_all", c] = [
            send(own, own, y_ss.at[1, c, step - 1], y_rs.at[1, c, step - 1], y_peer(step))
            for step in (1, 3, 2)
        ]
        pending["e", c] = [pass_on(c, y)]

    def y_all(c):
        for copy, step in zip(pending.pop(("y_all", c)), (1, 3, 2)):
            copy.wait_recv()
            pending["e", c].append(pass_on(c, turn(y, -step + 4)))

    def error_of(c, half, target):
        value = errs[c, half, :, 2 * target : 2 * target + 2].reshape(4, 2, 2, 2, 8, 128)
        sides = [value[:, :, :, side].reshape(4 * rows, 128) for side in range(2)]
        return jnp.concatenate(sides, axis=1)

    def back(c):
        arrive(("e", c))
        total = None
        for half in range(2):
            for target in range(2):
                value = split(error_of(c, half, target))
                part = product(value, (dec[half, target, 0], dec[half, target, 1]), NT)
                total = part if total is None else total + part
        back_part[c] = total.reshape(4, rows, 256)
        pending["back", c] = [
            send(
                back_part.at[c, turn(width, step)],
                back_recv.at[c, step - 1],
                x_ss.at[2, c, step - 1],
                x_rs.at[2, c, step - 1],
                x_peer(step),
            )
            for step in (1, 3, 2)
        ]

    def grad(c):
        if c % 2 == 0:
            return
        turned = split(acts[c - 1 : c + 1].reshape(8 * rows, 256).T)
        for target in range(2):
            for half in range(2):
                value = jnp.concatenate([error_of(c - 1, half, target), error_of(c, half, target)], axis=0)
                part = product(turned, split(value), NN)
                if target == 0:
                    part = jnp.where(layer == 0, part, 0.0)
                columns = slice(half * 256, (half + 1) * 256)
                if c == 1:
                    dec_grad_ref[target, :, columns] = part
                else:
                    dec_grad_ref[target, :, columns] += part

    def finish(c):
        arrive(("back", c))
        total = back_part[c, width] + (back_recv[c, 0] + back_recv[c, 1] + back_recv[c, 2])
        pre_grad_ref[c * rows : (c + 1) * rows, :] = total * slope[c]

    run = locals()
    stages = {name: run[name] for name, _ in STAGES}
    for name, c in stage_order(chunks):
        stages[name](c)
    for copy in sent:
        copy.wait_send()


def local(inputs, targets, w_enc, b_enc, thresholds, w_dec, b_dec):
    tokens, width = inputs.shape[1:]
    feats = w_enc.shape[2]
    c = CHUNKS
    rows = tokens // (NX * c)
    half = width // 2
    vmem = pl.BlockSpec(memory_space=pltpu.VMEM)
    hbm = pl.BlockSpec(memory_space=pltpu.HBM)
    dma = pltpu.SemaphoreType.DMA
    dec_grad, pre_grad = pl.pallas_call(
        kernel,
        out_shape=(
            jax.ShapeDtypeStruct(w_dec.shape[1:], F32),
            jax.ShapeDtypeStruct((tokens // NX, feats), F32),
        ),
        in_specs=[hbm] * 7,
        out_specs=(vmem, vmem),
        scratch_shapes=[
            pltpu.VMEM(targets.shape, F32),
            pltpu.VMEM((1, feats), F32),
            pltpu.VMEM((1, feats), F32),
            pltpu.VMEM(b_dec.shape, F32),
            pltpu.VMEM((NX, c, rows, width), F32),
            pltpu.VMEM((width, feats), F32),
            pltpu.VMEM((2, feats, width), F32),
            pltpu.VMEM((2, width, feats), BF16),
            pltpu.VMEM((2, 2, 2, feats, half), BF16),
            pltpu.VMEM((c, NX, rows, feats), F32),
            pltpu.VMEM((c, 3, rows, feats), F32),
            pltpu.VMEM((c, NX, rows, feats), F32),
            pltpu.VMEM((c, rows, feats), F32),
            pltpu.VMEM((c, NY, 2 * rows, half), F32),
            pltpu.VMEM((c, NY, 2 * rows, half), F32),
            pltpu.VMEM((c, NY, 2 * rows, half), F32),
            pltpu.VMEM((c, 3, 2 * rows, half), F32),
            pltpu.VMEM((c, 4, 2 * rows // 4, half), F32),
            pltpu.VMEM((c, 3, 2 * rows // 4, half), F32),
            pltpu.VMEM((c, 4, 8, 128), F32),
            pltpu.VMEM((c, 3, 8, 128), F32),
            pltpu.VMEM((c, 2, NY, 4, 4, 8, 128), F32),
            pltpu.VMEM((c, NX, rows, feats), F32),
            pltpu.VMEM((c, 3, rows, feats), F32),
            dma((6 + c,)),
            dma((3, c, 3)),
            dma((3, c, 3)),
            dma((2, c, 3)),
            dma((2, c, 3)),
            dma((2, c, 3)),
            dma((2, c, 3)),
            dma((2, c, 3)),
            dma((2, c, 3)),
            dma((2, c, 4)),
            dma((2, c, 4)),
        ],
        compiler_params=pltpu.CompilerParams(
            collective_id=0, has_side_effects=True, vmem_limit_bytes=54 * 1024 * 1024
        ),
    )(
        inputs.reshape(NX, c, rows, width),
        targets,
        w_enc[0],
        b_enc,
        thresholds,
        w_dec[0],
        b_dec,
    )
    return dec_grad[None], pre_grad[None]


def solution(mesh):
    in_specs = (
        P("layer", None, "width"),
        P(None, ("layer", "feat"), "width"),
        P("layer", "width", "feat"),
        P("layer", "feat"),
        P("layer", "feat"),
        P("layer", None, "feat", "width"),
        P(None, "width"),
    )
    out_specs = (P("layer", None, "feat", "width"), P("layer", "width", "feat"))
    return jax.shard_map(local, mesh=mesh, in_specs=in_specs, out_specs=out_specs, check_vma=False)
```

```python
import functools

import jax
import jax.numpy as jnp
from jax import lax
from jax.experimental import pallas as pl
from jax.experimental.pallas import tpu as pltpu
from jax.sharding import PartitionSpec as P

softness = 0.5
MESH = pl.DeviceIdType.MESH
CHUNKS = 8
SPACING = 3.5
NX = 4
NY = 4
NZ = 16
F32 = jnp.float32
BF16 = jnp.bfloat16

STAGES = (
    ("pre", 1.5),
    ("gate", 6.0),
    ("recon", 6.0),
    ("core_sum", 1.8),
    ("y_sum", 5.3),
    ("zlo_sum", 5.1),
    ("zhi_sum", 7.5),
    ("zhi_all", 7.5),
    ("zlo_all", 5.1),
    ("y_all", 5.3),
    ("back", 1.8),
    ("grad", 0.3),
    ("finish", 6.0),
)


def stage_order(chunks):
    ready = []
    for chunk in range(chunks):
        when = chunk * SPACING
        for place, (name, wait) in enumerate(STAGES):
            when += wait
            ready.append((when, place, chunk, name))
    return [(name, chunk) for _, _, chunk, name in sorted(ready)]


def split(value):
    high = value.astype(BF16)
    low = (value - high.astype(F32)).astype(BF16)
    return high, low


def product(a, b, dims):
    dot = functools.partial(
        lax.dot_general, dimension_numbers=(dims, ((), ())), preferred_element_type=F32
    )
    return dot(a[0], b[0]) + (dot(a[0], b[1]) + dot(a[1], b[0]))


NN = ((1,), (0,))
NT = ((1,), (1,))


def kernel(
    x_hbm,
    targets_hbm,
    enc_hbm,
    b_enc_hbm,
    thr_hbm,
    dec_hbm,
    b_dec_hbm,
    dec_grad_hbm,
    pre_grad_hbm,
    dec_grad_ref,
    pre_grad_ref,
    out_sem,
    targets_ref,
    b_enc_ref,
    thr_ref,
    b_dec_ref,
    x_ref,
    enc_f32,
    dec_f32,
    enc,
    dec,
    pre_part,
    pre_recv,
    acts,
    slope,
    q_send,
    q_own,
    q_recv,
    y_recv,
    zlo_part,
    zlo_recv,
    zhi_part,
    zhi_recv,
    errs,
    back_part,
    back_recv,
    load_sem,
    x_ss,
    x_rs,
    y_ss,
    y_rs,
    zlo_ss,
    zlo_rs,
    zhi_ss,
    zhi_rs,
    c_ss,
    c_rs,
):
    layer = lax.axis_index("layer")
    feat = lax.axis_index("feat")
    width = lax.axis_index("width")
    core = lax.rem(feat, 2)
    z = lax.rem(feat // 2, NZ)
    zlo = lax.rem(z, 4)
    zhi = z // 4
    y = (feat // (2 * NZ)) * 2 + layer
    chunks, _, rows, _ = acts.shape

    def turn(place, step):
        return lax.rem(place + step, 4)

    def device(y_at, z_at, core_at, x_at):
        return (lax.rem(y_at, 2), (y_at // 2) * (2 * NZ) + z_at * 2 + core_at, x_at)

    def x_peer(step):
        return device(y, z, core, turn(width, step))

    def y_peer(step):
        return device(turn(y, step), z, core, width)

    def zlo_peer(step):
        return device(y, zhi * 4 + turn(zlo, step), core, width)

    def zhi_peer(step):
        return device(y, turn(zhi, step) * 4 + zlo, core, width)

    partner = device(y, z, 1 - core, width)
    peers = [partner] + [peer(step) for peer in (x_peer, y_peer, zlo_peer, zhi_peer) for step in (1, 2, 3)]

    loads = [
        pltpu.make_async_copy(enc_hbm, enc_f32, load_sem.at[0]),
        pltpu.make_async_copy(dec_hbm, dec_f32, load_sem.at[1]),
    ]
    x_loads = [
        pltpu.make_async_copy(x_hbm.at[:, c], x_ref.at[:, c], load_sem.at[2 + c]) for c in range(chunks)
    ]
    small = ((b_enc_hbm, b_enc_ref), (thr_hbm, thr_ref), (targets_hbm, targets_ref), (b_dec_hbm, b_dec_ref))
    small_loads = [
        pltpu.make_async_copy(src, dst, load_sem.at[2 + chunks + place]) for place, (src, dst) in enumerate(small)
    ]
    for load in [loads[0], x_loads[0], *small_loads, loads[1], *x_loads[1:]]:
        load.start()
    barrier = pltpu.get_barrier_semaphore()
    for peer in peers:
        pl.semaphore_signal(barrier, inc=1, device_id=peer, device_id_type=MESH)

    sent = []
    stored = []

    def send(src, dst, send_sem, recv_sem, peer):
        copy = pltpu.make_async_remote_copy(
            src_ref=src,
            dst_ref=dst,
            send_sem=send_sem,
            recv_sem=recv_sem,
            device_id=peer,
            device_id_type=MESH,
        )
        copy.start()
        sent.append(copy)
        return copy

    pending = {}

    def arrive(key):
        for copy in pending.pop(key):
            copy.wait_recv()

    loads[0].wait()
    high, low = split(enc_f32[...])
    enc[0] = high
    enc[1] = low

    def load_dec():
        for target in range(2):
            for half in range(2):
                value = dec_f32[target, :, half * 256 : (half + 1) * 256]
                if target == 0:
                    value = jnp.where(layer == 0, value, 0.0)
                high, low = split(value)
                dec[half, target, 0] = high
                dec[half, target, 1] = low

    def pre(c):
        x_loads[c].wait()
        value = x_ref[:, c].reshape(4 * rows, x_ref.shape[3])
        part = product(split(value), (enc[0], enc[1]), NN)
        pre_part[c] = part.reshape(4, rows, 256)
        if c == 0:
            pl.semaphore_wait(barrier, len(peers))
        pending["pre", c] = [
            send(
                pre_part.at[c, turn(width, step)],
                pre_recv.at[c, step - 1],
                x_ss.at[0, c, step - 1],
                x_rs.at[0, c, step - 1],
                x_peer(step),
            )
            for step in (2, 1, 3)
        ]
        if c == 0:
            loads[1].wait()
            for load in small_loads:
                load.wait()
            load_dec()

    def gate(c):
        arrive(("pre", c))
        total = pre_part[c, width] + pre_recv[c, 0] + pre_recv[c, 1] + pre_recv[c, 2]
        total = total + b_enc_ref[...]
        opened = jax.nn.sigmoid((total - thr_ref[...]) / softness)
        acts[c, width] = total * opened
        slope[c] = opened + total * opened * (1.0 - opened) / softness
        pending["acts", c] = [
            send(
                acts.at[c, width],
                acts.at[c, width],
                x_ss.at[1, c, step - 1],
                x_rs.at[1, c, step - 1],
                x_peer(step),
            )
            for step in (2, 1, 3)
        ]

    first = (layer * 64 + feat) * targets_ref.shape[1]
    own_x = first // (rows * chunks)
    own_chunk = lax.rem(first, rows * chunks) // rows
    own_row = pl.multiple_of(lax.rem(first, rows), 8)

    def recon(c):
        arrive(("acts", c))
        value = split(acts[c].reshape(4 * rows, 256))
        for dst, half in ((q_send, 1 - core), (q_own, core)):
            for target in range(2):
                part = product(value, (dec[half, target, 0], dec[half, target, 1]), NN)
                dst[c, :, target * rows : (target + 1) * rows, :] = part.reshape(4, rows, 256)

            @pl.when(own_chunk == c)
            def _():
                for target in range(2):
                    at = pl.multiple_of(target * rows + own_row, 8)
                    spot = (c, own_x, pl.ds(at, 8), slice(None))
                    columns = pl.ds(pl.multiple_of(half * 256, 256), 256)
                    dst[spot] = dst[spot] - targets_ref[target, :, columns]

            if dst is q_send:
                pending["q", c] = [
                    send(q_send.at[c], q_recv.at[c], c_ss.at[0, c, 0], c_rs.at[0, c, 0], partner)
                ]

    def core_sum(c):
        arrive(("q", c))
        copies = []
        for step in (2, 1, 3):
            at = turn(y, step)
            q_own[c, at] = q_own[c, at] + q_recv[c, at]
            copies.append(
                send(
                    q_own.at[c, at],
                    y_recv.at[c, step - 1],
                    y_ss.at[0, c, step - 1],
                    y_rs.at[0, c, step - 1],
                    y_peer(step),
                )
            )
        pending["y", c] = copies

    def y_sum(c):
        arrive(("y", c))
        total = (q_own[c, y] + q_recv[c, y]) + (y_recv[c, 0] + y_recv[c, 1] + y_recv[c, 2])
        zlo_part[c] = total.reshape(4, 2 * rows // 4, 256)
        pending["zlo", c] = [
            send(
                zlo_part.at[c, turn(zlo, step)],
                zlo_recv.at[c, step - 1],
                zlo_ss.at[0, c, step - 1],
                zlo_rs.at[0, c, step - 1],
                zlo_peer(step),
            )
            for step in (2, 1, 3)
        ]

    def zlo_sum(c):
        arrive(("zlo", c))
        total = zlo_part[c, zlo] + (zlo_recv[c, 0] + zlo_recv[c, 1] + zlo_recv[c, 2])
        for part in range(4):
            down, across = (part // 2) * 8, (part % 2) * 128
            zhi_part[c, part] = total[down : down + 8, across : across + 128]
        pending["zhi", c] = [
            send(
                zhi_part.at[c, turn(zhi, step)],
                zhi_recv.at[c, step - 1],
                zhi_ss.at[0, c, step - 1],
                zhi_rs.at[0, c, step - 1],
                zhi_peer(step),
            )
            for step in (2, 1, 3)
        ]

    def zhi_sum(c):
        arrive(("zhi", c))
        total = zhi_part[c, zhi] + (zhi_recv[c, 0] + zhi_recv[c, 1] + zhi_recv[c, 2])
        columns = pl.ds(pl.multiple_of(core * 256 + lax.rem(zhi, 2) * 128, 128), 128)
        bias = b_dec_ref[:, columns]
        total = total + jnp.where(zlo >= 2, bias[1:2], bias[0:1])
        errs[c, core, y, zlo, zhi] = total
        own = errs.at[c, core, y, zlo, zhi]
        pending["zhi_all", c] = [
            send(own, own, zhi_ss.at[1, c, step - 1], zhi_rs.at[1, c, step - 1], zhi_peer(step))
            for step in (2, 1, 3)
        ]

    def zhi_all(c):
        arrive(("zhi_all", c))
        own = errs.at[c, core, y, zlo]
        pending["zlo_all", c] = [
            send(own, own, zlo_ss.at[1, c, step - 1], zlo_rs.at[1, c, step - 1], zlo_peer(step))
            for step in (2, 1, 3)
        ]

    def pass_on(c, at):
        own = errs.at[c, core, at]
        return send(own, own, c_ss.at[1, c, at], c_rs.at[1, c, at], partner)

    def zlo_all(c):
        arrive(("zlo_all", c))
        own = errs.at[c, core, y]
        pending["y_all", c] = [
            send(own, own, y_ss.at[1, c, step - 1], y_rs.at[1, c, step - 1], y_peer(step))
            for step in (2, 1, 3)
        ]
        pending["e", c] = [pass_on(c, y)]

    def y_all(c):
        for copy, step in zip(pending.pop(("y_all", c)), (2, 1, 3)):
            copy.wait_recv()
            pending["e", c].append(pass_on(c, turn(y, -step + 4)))

    def error_of(c, half, target):
        value = errs[c, half, :, 2 * target : 2 * target + 2].reshape(4, 2, 2, 2, 8, 128)
        sides = [value[:, :, :, side].reshape(4 * rows, 128) for side in range(2)]
        return jnp.concatenate(sides, axis=1)

    def back(c):
        arrive(("e", c))
        total = None
        for half in range(2):
            for target in range(2):
                value = split(error_of(c, half, target))
                part = product(value, (dec[half, target, 0], dec[half, target, 1]), NT)
                total = part if total is None else total + part
        back_part[c] = total.reshape(4, rows, 256)
        pending["back", c] = [
            send(
                back_part.at[c, turn(width, step)],
                back_recv.at[c, step - 1],
                x_ss.at[2, c, step - 1],
                x_rs.at[2, c, step - 1],
                x_peer(step),
            )
            for step in (2, 1, 3)
        ]

    def grad(c):
        if c % 2 == 0:
            return
        turned = split(acts[c - 1 : c + 1].reshape(8 * rows, 256).T)
        for target in range(2):
            for half in range(2):
                value = jnp.concatenate([error_of(c - 1, half, target), error_of(c, half, target)], axis=0)
                part = product(turned, split(value), NN)
                if target == 0:
                    part = jnp.where(layer == 0, part, 0.0)
                columns = slice(half * 256, (half + 1) * 256)
                if c == 1:
                    dec_grad_ref[target, :, columns] = part
                else:
                    dec_grad_ref[target, :, columns] += part
            if c == chunks - 1:
                copy = pltpu.make_async_copy(dec_grad_ref.at[target], dec_grad_hbm.at[target], out_sem.at[target])
                copy.start()
                stored.append(copy)

    def finish(c):
        arrive(("back", c))
        total = back_part[c, width] + (back_recv[c, 0] + back_recv[c, 1] + back_recv[c, 2])
        pre_grad_ref[c] = total * slope[c]
        copy = pltpu.make_async_copy(
            pre_grad_ref.at[c], pre_grad_hbm.at[c * rows : (c + 1) * rows], out_sem.at[2 + c]
        )
        copy.start()
        stored.append(copy)

    run = locals()
    stages = {name: run[name] for name, _ in STAGES}
    for name, c in stage_order(chunks):
        stages[name](c)
    for copy in sent:
        copy.wait_send()
    for copy in stored:
        copy.wait()


def settle(*refs):
    count = len(refs) // 3
    sources, results, held = refs[:count], refs[count : 2 * count], refs[2 * count : 3 * count]
    in_sem, out_sem = refs[3 * count :]
    pieces = []
    for source, result, hold in zip(sources, results, held):
        step = 64
        for start in range(0, source.shape[0], step):
            at = slice(start, start + step)
            n = len(pieces)
            pieces.append(
                (
                    pltpu.make_async_copy(source.at[at], hold.at[at], in_sem.at[n]),
                    pltpu.make_async_copy(hold.at[at], result.at[at], out_sem.at[n]),
                )
            )
    for load, _ in pieces:
        load.start()
    for load, store in pieces:
        load.wait()
        store.start()
    for _, store in pieces:
        store.wait()


def local(inputs, targets, w_enc, b_enc, thresholds, w_dec, b_dec):
    tokens, width = inputs.shape[1:]
    feats = w_enc.shape[2]
    c = CHUNKS
    rows = tokens // (NX * c)
    half = width // 2
    hbm = pl.BlockSpec(memory_space=pltpu.HBM)
    dma = pltpu.SemaphoreType.DMA
    dec_grad, pre_grad = pl.pallas_call(
        kernel,
        out_shape=(
            jax.ShapeDtypeStruct(w_dec.shape[1:], F32),
            jax.ShapeDtypeStruct((tokens // NX, feats), F32),
        ),
        in_specs=[hbm] * 7,
        out_specs=(hbm, hbm),
        scratch_shapes=[
            pltpu.VMEM(w_dec.shape[1:], F32),
            pltpu.VMEM((c, rows, feats), F32),
            dma((2 + c,)),
            pltpu.VMEM(targets.shape, F32),
            pltpu.VMEM((1, feats), F32),
            pltpu.VMEM((1, feats), F32),
            pltpu.VMEM(b_dec.shape, F32),
            pltpu.VMEM((NX, c, rows, width), F32),
            pltpu.VMEM((width, feats), F32),
            pltpu.VMEM((2, feats, width), F32),
            pltpu.VMEM((2, width, feats), BF16),
            pltpu.VMEM((2, 2, 2, feats, half), BF16),
            pltpu.VMEM((c, NX, rows, feats), F32),
            pltpu.VMEM((c, 3, rows, feats), F32),
            pltpu.VMEM((c, NX, rows, feats), F32),
            pltpu.VMEM((c, rows, feats), F32),
            pltpu.VMEM((c, NY, 2 * rows, half), F32),
            pltpu.VMEM((c, NY, 2 * rows, half), F32),
            pltpu.VMEM((c, NY, 2 * rows, half), F32),
            pltpu.VMEM((c, 3, 2 * rows, half), F32),
            pltpu.VMEM((c, 4, 2 * rows // 4, half), F32),
            pltpu.VMEM((c, 3, 2 * rows // 4, half), F32),
            pltpu.VMEM((c, 4, 8, 128), F32),
            pltpu.VMEM((c, 3, 8, 128), F32),
            pltpu.VMEM((c, 2, NY, 4, 4, 8, 128), F32),
            pltpu.VMEM((c, NX, rows, feats), F32),
            pltpu.VMEM((c, 3, rows, feats), F32),
            dma((6 + c,)),
            dma((3, c, 3)),
            dma((3, c, 3)),
            dma((2, c, 3)),
            dma((2, c, 3)),
            dma((2, c, 3)),
            dma((2, c, 3)),
            dma((2, c, 3)),
            dma((2, c, 3)),
            dma((2, c, 4)),
            dma((2, c, 4)),
        ],
        compiler_params=pltpu.CompilerParams(
            collective_id=0, has_side_effects=True, vmem_limit_bytes=54 * 1024 * 1024
        ),
    )(
        inputs.reshape(NX, c, rows, width),
        targets,
        w_enc[0],
        b_enc,
        thresholds,
        w_dec[0],
        b_dec,
    )
    parts = (dec_grad.reshape(2 * feats, width), pre_grad)
    count = sum(part.shape[0] for part in parts) // 64
    dec_grad, pre_grad = pl.pallas_call(
        settle,
        out_shape=tuple(jax.ShapeDtypeStruct(part.shape, F32) for part in parts),
        in_specs=[hbm] * 2,
        out_specs=(hbm,) * 2,
        scratch_shapes=[pltpu.VMEM(part.shape, F32) for part in parts] + [dma((count,)), dma((count,))],
    )(*parts)
    return dec_grad.reshape(w_dec.shape), pre_grad[None]


def solution(mesh):
    in_specs = (
        P("layer", None, "width"),
        P(None, ("layer", "feat"), "width"),
        P("layer", "width", "feat"),
        P("layer", "feat"),
        P("layer", "feat"),
        P("layer", None, "feat", "width"),
        P(None, "width"),
    )
    out_specs = (P("layer", None, "feat", "width"), P("layer", "width", "feat"))
    return jax.shard_map(local, mesh=mesh, in_specs=in_specs, out_specs=out_specs, check_vma=False)
```

```python
import functools

import jax
import jax.numpy as jnp
from jax import lax
from jax.experimental import pallas as pl
from jax.experimental.pallas import tpu as pltpu
from jax.sharding import PartitionSpec as P

softness = 0.5
MESH = pl.DeviceIdType.MESH
CHUNKS = 8
SPACING = 3.5
NX = 4
NY = 4
NZ = 16
F32 = jnp.float32
BF16 = jnp.bfloat16

STAGES = (
    ("pre", 1.5),
    ("gate", 6.0),
    ("recon", 6.0),
    ("core_sum", 2.8),
    ("y_sum", 5.3),
    ("zlo_sum", 5.1),
    ("zhi_sum", 7.5),
    ("zhi_all", 7.5),
    ("zlo_all", 5.1),
    ("y_all", 5.3),
    ("back", 2.8),
    ("grad", 0.3),
    ("finish", 6.0),
)


def stage_order(chunks):
    ready = []
    for chunk in range(chunks):
        when = chunk * SPACING
        for place, (name, wait) in enumerate(STAGES):
            when += wait
            ready.append((when, place, chunk, name))
    return [(name, chunk) for _, _, chunk, name in sorted(ready)]


def split(value):
    high = value.astype(BF16)
    low = (value - high.astype(F32)).astype(BF16)
    return high, low


def product(a, b, dims):
    dot = functools.partial(
        lax.dot_general, dimension_numbers=(dims, ((), ())), preferred_element_type=F32
    )
    return dot(a[0], b[0]) + (dot(a[0], b[1]) + dot(a[1], b[0]))


NN = ((1,), (0,))
NT = ((1,), (1,))


def kernel(
    x_hbm,
    targets_hbm,
    enc_hbm,
    b_enc_hbm,
    thr_hbm,
    dec_hbm,
    b_dec_hbm,
    dec_grad_hbm,
    pre_grad_hbm,
    dec_grad_ref,
    pre_grad_ref,
    out_sem,
    targets_ref,
    b_enc_ref,
    thr_ref,
    b_dec_ref,
    x_ref,
    enc_f32,
    dec_f32,
    enc,
    dec,
    pre_part,
    pre_recv,
    acts,
    slope,
    q_send,
    q_own,
    q_recv,
    y_recv,
    zlo_part,
    zlo_recv,
    zhi_part,
    zhi_recv,
    errs,
    back_part,
    back_recv,
    load_sem,
    x_ss,
    x_rs,
    y_ss,
    y_rs,
    zlo_ss,
    zlo_rs,
    zhi_ss,
    zhi_rs,
    c_ss,
    c_rs,
):
    layer = lax.axis_index("layer")
    feat = lax.axis_index("feat")
    width = lax.axis_index("width")
    core = lax.rem(feat, 2)
    z = lax.rem(feat // 2, NZ)
    zlo = lax.rem(z, 4)
    zhi = z // 4
    y = (feat // (2 * NZ)) * 2 + layer
    chunks, _, rows, _ = acts.shape

    def turn(place, step):
        return lax.rem(place + step, 4)

    def device(y_at, z_at, core_at, x_at):
        return (lax.rem(y_at, 2), (y_at // 2) * (2 * NZ) + z_at * 2 + core_at, x_at)

    def x_peer(step):
        return device(y, z, core, turn(width, step))

    def y_peer(step):
        return device(turn(y, step), z, core, width)

    def zlo_peer(step):
        return device(y, zhi * 4 + turn(zlo, step), core, width)

    def zhi_peer(step):
        return device(y, turn(zhi, step) * 4 + zlo, core, width)

    partner = device(y, z, 1 - core, width)
    peers = [partner] + [peer(step) for peer in (x_peer, y_peer, zlo_peer, zhi_peer) for step in (1, 2, 3)]

    loads = [
        pltpu.make_async_copy(enc_hbm, enc_f32, load_sem.at[0]),
        pltpu.make_async_copy(dec_hbm, dec_f32, load_sem.at[1]),
    ]
    x_loads = [
        pltpu.make_async_copy(x_hbm.at[:, c], x_ref.at[:, c], load_sem.at[2 + c]) for c in range(chunks)
    ]
    small = ((b_enc_hbm, b_enc_ref), (thr_hbm, thr_ref), (targets_hbm, targets_ref), (b_dec_hbm, b_dec_ref))
    small_loads = [
        pltpu.make_async_copy(src, dst, load_sem.at[2 + chunks + place]) for place, (src, dst) in enumerate(small)
    ]
    for load in [loads[0], x_loads[0], *small_loads, loads[1], *x_loads[1:]]:
        load.start()
    barrier = pltpu.get_barrier_semaphore()
    for peer in peers:
        pl.semaphore_signal(barrier, inc=1, device_id=peer, device_id_type=MESH)

    sent = []
    stored = []

    def send(src, dst, send_sem, recv_sem, peer):
        copy = pltpu.make_async_remote_copy(
            src_ref=src,
            dst_ref=dst,
            send_sem=send_sem,
            recv_sem=recv_sem,
            device_id=peer,
            device_id_type=MESH,
        )
        copy.start()
        sent.append(copy)
        return copy

    pending = {}

    def arrive(key):
        for copy in pending.pop(key):
            copy.wait_recv()

    loads[0].wait()
    high, low = split(enc_f32[...])
    enc[0] = high
    enc[1] = low

    def load_dec():
        for target in range(2):
            for half in range(2):
                value = dec_f32[target, :, half * 256 : (half + 1) * 256]
                if target == 0:
                    value = jnp.where(layer == 0, value, 0.0)
                high, low = split(value)
                dec[half, target, 0] = high
                dec[half, target, 1] = low

    def pre(c):
        x_loads[c].wait()
        value = x_ref[:, c].reshape(4 * rows, x_ref.shape[3])
        part = product(split(value), (enc[0], enc[1]), NN)
        pre_part[c] = part.reshape(4, rows, 256)
        if c == 0:
            pl.semaphore_wait(barrier, len(peers))
        pending["pre", c] = [
            send(
                pre_part.at[c, turn(width, step)],
                pre_recv.at[c, step - 1],
                x_ss.at[0, c, step - 1],
                x_rs.at[0, c, step - 1],
                x_peer(step),
            )
            for step in (2, 1, 3)
        ]
        if c == 0:
            loads[1].wait()
            for load in small_loads:
                load.wait()
            load_dec()

    def gate(c):
        arrive(("pre", c))
        total = pre_part[c, width] + pre_recv[c, 0] + pre_recv[c, 1] + pre_recv[c, 2]
        total = total + b_enc_ref[...]
        opened = jax.nn.sigmoid((total - thr_ref[...]) / softness)
        acts[c, width] = total * opened
        slope[c] = opened + total * opened * (1.0 - opened) / softness
        pending["acts", c] = [
            send(
                acts.at[c, width],
                acts.at[c, width],
                x_ss.at[1, c, step - 1],
                x_rs.at[1, c, step - 1],
                x_peer(step),
            )
            for step in (2, 1, 3)
        ]

    first = (layer * 64 + feat) * targets_ref.shape[1]
    own_x = first // (rows * chunks)
    own_chunk = lax.rem(first, rows * chunks) // rows
    own_row = pl.multiple_of(lax.rem(first, rows), 8)

    def recon(c):
        arrive(("acts", c))
        value = split(acts[c].reshape(4 * rows, 256))
        for dst, half in ((q_send, 1 - core), (q_own, core)):
            for target in range(2):
                part = product(value, (dec[half, target, 0], dec[half, target, 1]), NN)
                dst[c, :, target * rows : (target + 1) * rows, :] = part.reshape(4, rows, 256)

            @pl.when(own_chunk == c)
            def _():
                for target in range(2):
                    at = pl.multiple_of(target * rows + own_row, 8)
                    spot = (c, own_x, pl.ds(at, 8), slice(None))
                    columns = pl.ds(pl.multiple_of(half * 256, 256), 256)
                    dst[spot] = dst[spot] - targets_ref[target, :, columns]

            if dst is q_send:
                pending["q", c] = [
                    send(q_send.at[c], q_recv.at[c], c_ss.at[0, c, 0], c_rs.at[0, c, 0], partner)
                ]

    def core_sum(c):
        arrive(("q", c))
        copies = []
        for step in (2, 1, 3):
            at = turn(y, step)
            q_own[c, at] = q_own[c, at] + q_recv[c, at]
            copies.append(
                send(
                    q_own.at[c, at],
                    y_recv.at[c, step - 1],
                    y_ss.at[0, c, step - 1],
                    y_rs.at[0, c, step - 1],
                    y_peer(step),
                )
            )
        pending["y", c] = copies

    def y_sum(c):
        arrive(("y", c))
        total = (q_own[c, y] + q_recv[c, y]) + (y_recv[c, 0] + y_recv[c, 1] + y_recv[c, 2])
        zlo_part[c] = total.reshape(4, 2 * rows // 4, 256)
        pending["zlo", c] = [
            send(
                zlo_part.at[c, turn(zlo, step)],
                zlo_recv.at[c, step - 1],
                zlo_ss.at[0, c, step - 1],
                zlo_rs.at[0, c, step - 1],
                zlo_peer(step),
            )
            for step in (2, 1, 3)
        ]

    def zlo_sum(c):
        arrive(("zlo", c))
        total = zlo_part[c, zlo] + (zlo_recv[c, 0] + zlo_recv[c, 1] + zlo_recv[c, 2])
        for part in range(4):
            down, across = (part // 2) * 8, (part % 2) * 128
            zhi_part[c, part] = total[down : down + 8, across : across + 128]
        pending["zhi", c] = [
            send(
                zhi_part.at[c, turn(zhi, step)],
                zhi_recv.at[c, step - 1],
                zhi_ss.at[0, c, step - 1],
                zhi_rs.at[0, c, step - 1],
                zhi_peer(step),
            )
            for step in (2, 1, 3)
        ]

    def zhi_sum(c):
        arrive(("zhi", c))
        total = zhi_part[c, zhi] + (zhi_recv[c, 0] + zhi_recv[c, 1] + zhi_recv[c, 2])
        columns = pl.ds(pl.multiple_of(core * 256 + lax.rem(zhi, 2) * 128, 128), 128)
        bias = b_dec_ref[:, columns]
        total = total + jnp.where(zlo >= 2, bias[1:2], bias[0:1])
        errs[c, core, y, zlo, zhi] = total
        own = errs.at[c, core, y, zlo, zhi]
        pending["zhi_all", c] = [
            send(own, own, zhi_ss.at[1, c, step - 1], zhi_rs.at[1, c, step - 1], zhi_peer(step))
            for step in (2, 1, 3)
        ]

    def zhi_all(c):
        arrive(("zhi_all", c))
        own = errs.at[c, core, y, zlo]
        pending["zlo_all", c] = [
            send(own, own, zlo_ss.at[1, c, step - 1], zlo_rs.at[1, c, step - 1], zlo_peer(step))
            for step in (2, 1, 3)
        ]

    def pass_on(c, at):
        own = errs.at[c, core, at]
        return send(own, own, c_ss.at[1, c, at], c_rs.at[1, c, at], partner)

    def zlo_all(c):
        arrive(("zlo_all", c))
        own = errs.at[c, core, y]
        pending["y_all", c] = [
            send(own, own, y_ss.at[1, c, step - 1], y_rs.at[1, c, step - 1], y_peer(step))
            for step in (2, 1, 3)
        ]
        pending["e", c] = [pass_on(c, y)]

    def y_all(c):
        for copy, step in zip(pending.pop(("y_all", c)), (2, 1, 3)):
            copy.wait_recv()
            pending["e", c].append(pass_on(c, turn(y, -step + 4)))

    def error_of(c, half, target):
        value = errs[c, half, :, 2 * target : 2 * target + 2].reshape(4, 2, 2, 2, 8, 128)
        sides = [value[:, :, :, side].reshape(4 * rows, 128) for side in range(2)]
        return jnp.concatenate(sides, axis=1)

    def back(c):
        arrive(("e", c))
        total = None
        for half in range(2):
            for target in range(2):
                value = split(error_of(c, half, target))
                part = product(value, (dec[half, target, 0], dec[half, target, 1]), NT)
                total = part if total is None else total + part
        back_part[c] = total.reshape(4, rows, 256)
        pending["back", c] = [
            send(
                back_part.at[c, turn(width, step)],
                back_recv.at[c, step - 1],
                x_ss.at[2, c, step - 1],
                x_rs.at[2, c, step - 1],
                x_peer(step),
            )
            for step in (2, 1, 3)
        ]

    def grad(c):
        if c % 2 == 0:
            return
        turned = split(acts[c - 1 : c + 1].reshape(8 * rows, 256).T)
        for target in range(2):
            for half in range(2):
                value = jnp.concatenate([error_of(c - 1, half, target), error_of(c, half, target)], axis=0)
                part = product(turned, split(value), NN)
                if target == 0:
                    part = jnp.where(layer == 0, part, 0.0)
                columns = slice(half * 256, (half + 1) * 256)
                if c == 1:
                    dec_grad_ref[target, :, columns] = part
                else:
                    dec_grad_ref[target, :, columns] += part
    def finish(c):
        if c == chunks - 1:
            for target in range(2):
                copy = pltpu.make_async_copy(dec_grad_ref.at[target], dec_grad_hbm.at[target], out_sem.at[target])
                copy.start()
                stored.append(copy)
        arrive(("back", c))
        total = back_part[c, width] + (back_recv[c, 0] + back_recv[c, 1] + back_recv[c, 2])
        pre_grad_ref[c] = total * slope[c]
        copy = pltpu.make_async_copy(
            pre_grad_ref.at[c], pre_grad_hbm.at[c * rows : (c + 1) * rows], out_sem.at[2 + c]
        )
        copy.start()
        stored.append(copy)

    run = locals()
    stages = {name: run[name] for name, _ in STAGES}
    for name, c in stage_order(chunks):
        stages[name](c)
    for copy in sent:
        copy.wait_send()
    for copy in stored:
        copy.wait()


def settle(*refs):
    count = len(refs) // 3
    sources, results, held = refs[:count], refs[count : 2 * count], refs[2 * count : 3 * count]
    in_sem, out_sem = refs[3 * count :]
    pieces = []
    for source, result, hold in zip(sources, results, held):
        step = 64
        for start in range(0, source.shape[0], step):
            at = slice(start, start + step)
            n = len(pieces)
            pieces.append(
                (
                    pltpu.make_async_copy(source.at[at], hold.at[at], in_sem.at[n]),
                    pltpu.make_async_copy(hold.at[at], result.at[at], out_sem.at[n]),
                )
            )
    for load, _ in pieces:
        load.start()
    for load, store in pieces:
        load.wait()
        store.start()
    for _, store in pieces:
        store.wait()


def local(inputs, targets, w_enc, b_enc, thresholds, w_dec, b_dec):
    tokens, width = inputs.shape[1:]
    feats = w_enc.shape[2]
    c = CHUNKS
    rows = tokens // (NX * c)
    half = width // 2
    hbm = pl.BlockSpec(memory_space=pltpu.HBM)
    dma = pltpu.SemaphoreType.DMA
    dec_grad, pre_grad = pl.pallas_call(
        kernel,
        out_shape=(
            jax.ShapeDtypeStruct(w_dec.shape[1:], F32),
            jax.ShapeDtypeStruct((tokens // NX, feats), F32),
        ),
        in_specs=[hbm] * 7,
        out_specs=(hbm, hbm),
        scratch_shapes=[
            pltpu.VMEM(w_dec.shape[1:], F32),
            pltpu.VMEM((c, rows, feats), F32),
            dma((2 + c,)),
            pltpu.VMEM(targets.shape, F32),
            pltpu.VMEM((1, feats), F32),
            pltpu.VMEM((1, feats), F32),
            pltpu.VMEM(b_dec.shape, F32),
            pltpu.VMEM((NX, c, rows, width), F32),
            pltpu.VMEM((width, feats), F32),
            pltpu.VMEM((2, feats, width), F32),
            pltpu.VMEM((2, width, feats), BF16),
            pltpu.VMEM((2, 2, 2, feats, half), BF16),
            pltpu.VMEM((c, NX, rows, feats), F32),
            pltpu.VMEM((c, 3, rows, feats), F32),
            pltpu.VMEM((c, NX, rows, feats), F32),
            pltpu.VMEM((c, rows, feats), F32),
            pltpu.VMEM((c, NY, 2 * rows, half), F32),
            pltpu.VMEM((c, NY, 2 * rows, half), F32),
            pltpu.VMEM((c, NY, 2 * rows, half), F32),
            pltpu.VMEM((c, 3, 2 * rows, half), F32),
            pltpu.VMEM((c, 4, 2 * rows // 4, half), F32),
            pltpu.VMEM((c, 3, 2 * rows // 4, half), F32),
            pltpu.VMEM((c, 4, 8, 128), F32),
            pltpu.VMEM((c, 3, 8, 128), F32),
            pltpu.VMEM((c, 2, NY, 4, 4, 8, 128), F32),
            pltpu.VMEM((c, NX, rows, feats), F32),
            pltpu.VMEM((c, 3, rows, feats), F32),
            dma((6 + c,)),
            dma((3, c, 3)),
            dma((3, c, 3)),
            dma((2, c, 3)),
            dma((2, c, 3)),
            dma((2, c, 3)),
            dma((2, c, 3)),
            dma((2, c, 3)),
            dma((2, c, 3)),
            dma((2, c, 4)),
            dma((2, c, 4)),
        ],
        compiler_params=pltpu.CompilerParams(
            collective_id=0, has_side_effects=True, vmem_limit_bytes=54 * 1024 * 1024
        ),
    )(
        inputs.reshape(NX, c, rows, width),
        targets,
        w_enc[0],
        b_enc,
        thresholds,
        w_dec[0],
        b_dec,
    )
    parts = (dec_grad.reshape(2 * feats, width), pre_grad)
    count = sum(part.shape[0] for part in parts) // 64
    dec_grad, pre_grad = pl.pallas_call(
        settle,
        out_shape=tuple(jax.ShapeDtypeStruct(part.shape, F32) for part in parts),
        in_specs=[hbm] * 2,
        out_specs=(hbm,) * 2,
        scratch_shapes=[pltpu.VMEM(part.shape, F32) for part in parts] + [dma((count,)), dma((count,))],
    )(*parts)
    return dec_grad.reshape(w_dec.shape), pre_grad[None]


def solution(mesh):
    in_specs = (
        P("layer", None, "width"),
        P(None, ("layer", "feat"), "width"),
        P("layer", "width", "feat"),
        P("layer", "feat"),
        P("layer", "feat"),
        P("layer", None, "feat", "width"),
        P(None, "width"),
    )
    out_specs = (P("layer", None, "feat", "width"), P("layer", "width", "feat"))
    return jax.shard_map(local, mesh=mesh, in_specs=in_specs, out_specs=out_specs, check_vma=False)
```
